128 devices in a mesh: row: 64 (over y_hi, z, x, core), rep: 2 (over y_lo).
Axes of the slice: x: 4, y: 4 (y_hi: 2, y_lo: 2; y = y_hi * 2 + y_lo), z: 4, core: 2. Of those that a mesh axis runs over, the one named last changes fastest.
Arguments:
- features: bfloat16 [131072, 256], P('row'), may hold values from -6 to 6
- adjacency: bfloat16 [1024, 48, 128, 128], P('row', 'rep'), may hold values from 0 to 3, as said below
- columns: int32 [1024, 48], P('row', 'rep'), may hold values from 0 to 1023, as said below
- live: int32 [1024], P('row'), may hold values from 0 to 48, as said below
- w_self: bfloat16 [256, 256], replicated, may hold values from -0.375 to 0.375
- w_neigh: bfloat16 [256, 256], replicated, may hold values from -4 to 4
- bias: float32 [256], replicated, may hold values from -3 to 3
Outputs:
- mixed: bfloat16 [131072, 256], P(('row', 'rep'))
The draws below stay inside these ranges and needn't reach their ends.
Inputs may be any that keep to these rules, and one draw needn't show every extreme that they name: `adjacency`: edge weights are nonnegative; most entries are zero, and some nodes have no edges at all. `columns`: the column block of every slot of block row b lies in the block rows held by a row index at most 2 away from the one holding b (never outside the graph). Slots at or after live[b] are ignored; some block row uses all 48 slots.
All inputs are finite; a program needn't handle non-finite values.
Results may differ from the reference program's by a relative error of at most 0.0048.
Values may be sent and summed in bfloat16 or wider, within the bound.
A program may use at most 64 MiB of HBM per device.

```python
import math
import jax
import jax.numpy as jnp
from jax import lax

F = 256
BLOCK = 128
NB_DEV = 16
K = 48
REACH = 2
NBLK = 1024
NODES = 131072


def draw_adjacency(key, part):
    first_key, second_key = jax.random.split(key, 2)
    uniform_draw = jax.random.uniform(first_key, (NBLK, K, BLOCK, BLOCK), jnp.float32)
    present = uniform_draw < 0.025
    scaled = uniform_draw / 0.025
    keep_rows = jax.random.randint(second_key, (NBLK, 1, BLOCK, 1), 0, 64) > 0
    weights = 0.1 * jnp.exp(scaled * math.log(30.0))
    weights = jnp.minimum(weights, 3.0)
    return jnp.where(present & keep_rows, weights, 0.0).astype(jnp.bfloat16)


def draw_columns(key, part):
    first_key, second_key = jax.random.split(key, 2)
    device_count = NBLK // NB_DEV
    block_ids = jnp.arange(NBLK, dtype=jnp.int32)[:, None]
    holder = block_ids // NB_DEV
    jumps = jax.random.randint(first_key, (NBLK, K), -REACH, REACH + 1)
    target = jnp.clip(holder + jumps, 0, device_count - 1)
    inside = jax.random.randint(second_key, (NBLK, K), 0, NB_DEV)
    return (target * NB_DEV + inside).astype(jnp.int32)


def draw_live(key, part):
    first_key, second_key, third_key = jax.random.split(key, 3)
    device_count = NBLK // NB_DEV
    levels = jax.random.randint(first_key, (device_count,), 0, 4)
    capacity = jnp.maximum(K // jnp.left_shift(1, levels), 1)
    capacity_rows = jnp.repeat(capacity, NB_DEV)
    spread_bits = jax.random.randint(second_key, (NBLK,), 0, 1 << 20)
    lowest = capacity_rows // 2
    counts = lowest + spread_bits % (capacity_rows - lowest + 1)
    full_row = jax.random.randint(third_key, (), 0, NBLK)
    return jnp.where(jnp.arange(NBLK, dtype=jnp.int32) == full_row, K, counts).astype(jnp.int32)


def level_of(rng, dims, cuts, low, top_value):
    def one(position, shards_of):
        draws = jax.random.uniform(jax.random.fold_in(jax.random.fold_in(rng, 6), position), (shards_of,), jnp.float32, low / len(cuts), top_value / len(cuts))
        return jnp.repeat(jnp.exp(draws), dims[position] // shards_of).reshape((-1,) + (1,) * (len(dims) - position - 1))

    gain = one(*cuts[0])
    for cut in cuts[1:]:
        gain = gain * one(*cut)
    return gain


def gaussian(rng, extent, scale, most, shards=(), kind=jnp.bfloat16):
    drawn = jax.random.normal(rng, extent, jnp.float32) * scale
    if len(shards) > 0:
        drawn = level_of(rng, extent, shards, -0.22, 0.18) * drawn
    return jnp.clip(drawn, min=-most, max=most).astype(kind)


def setup_inputs(seed: int = 0) -> dict:
    splits = jax.random.split(jax.random.key(seed), 8)
    features = gaussian(splits[0], (NODES, F), 1.0, 6.0, ((0, 64),))
    adjacency = draw_adjacency(jax.random.fold_in(splits[7], 71), 0)
    columns = draw_columns(jax.random.fold_in(splits[7], 71), 0)
    live = draw_live(jax.random.fold_in(splits[7], 71), 0)
    w_self = gaussian(splits[4], (F, F), F ** -0.5, 0.375)
    w_neigh = gaussian(splits[5], (F, F), 1.0, 4.0)
    bias = gaussian(splits[6], (F,), 0.5, 3.0, (), jnp.float32)
    return {"features": features, "adjacency": adjacency, "columns": columns, "live": live, "w_self": w_self, "w_neigh": w_neigh, "bias": bias}


def reference(features, adjacency, columns, live, w_self, w_neigh, bias):
    feature_blocks = features.reshape(NBLK, BLOCK, F)
    slot_ids = jnp.arange(K, dtype=jnp.int32)

    def one_row(row_item):
        row_tiles, row_columns, row_count = row_item
        live_slots = slot_ids < row_count
        masked = jnp.where(live_slots[:, None, None], row_tiles.astype(jnp.float32), jnp.float32(0.0))
        source = feature_blocks[row_columns.astype(jnp.int32)].astype(jnp.float32)
        running = jnp.einsum("sij,sjf->if", masked, source)
        degree = jnp.sum(masked, axis=(0, 2))
        return running, degree

    totals, degrees = lax.map(one_row, (adjacency, columns, live))
    totals = totals.reshape(NODES, F)
    degrees = degrees.reshape(NODES)
    neighbor_mean = (totals / jnp.maximum(degrees, jnp.float32(1.0))[:, None]).astype(jnp.bfloat16)
    summed = jnp.dot(features, w_self, preferred_element_type=jnp.float32)
    summed = summed + jnp.dot(neighbor_mean, w_neigh, preferred_element_type=jnp.float32) + bias
    return jax.nn.relu(summed).astype(jnp.bfloat16)
```

```python
import functools

import jax
import jax.numpy as jnp
from jax import lax
from jax.experimental import pallas as pl
from jax.experimental.pallas import tpu as pltpu
from jax.sharding import PartitionSpec as P

REACH = 2
LANES = 128
PIECES = 4
MESH = pl.DeviceIdType.MESH


def kernel(
    row_total, feats, adjacency, columns, live, w_self, w_neigh, bias, out,
    win_low, win_high, tiles, partial_out, partial_in, own_totals, base, inverse, degree_out, degree_in,
    tile_sem, own_sem, send_sem, recv_sem, part_send, part_recv, degree_sems,
):
    block_rows, slots, edge, _ = tiles.shape
    width = feats.shape[2]
    chunks = width // LANES
    piece = block_rows // PIECES
    half = block_rows // 2
    zero_block = (2 * REACH + 1) * block_rows
    win = (win_low, win_high)

    me = lax.axis_index("row")
    rep = lax.axis_index("rep")
    core = lax.rem(me, 2)
    mate = me + 1 - 2 * core
    other = 1 - rep
    has_next = me + 2 < row_total
    has_prev = me >= 2
    chip = me // 2
    middle = row_total // 4
    rep_next = jnp.where(chip == middle - 1, other, rep)
    rep_prev = jnp.where(chip == middle, other, rep)
    relay_out = jnp.where(core == 0, me + 2 < row_total, me >= 2)
    relay_in = jnp.where(core == 0, me >= 2, me + 2 < row_total)

    def tile_copy(b):
        return pltpu.make_async_copy(adjacency.at[b], tiles.at[b], tile_sem.at[b])

    def own_copy(c):
        return pltpu.make_async_copy(
            feats.at[:, :, pl.ds(c * LANES, LANES)],
            win[c].at[pl.ds(REACH * block_rows, block_rows)],
            own_sem.at[c],
        )

    def remote(flow, c, k, src, slot, device):
        return pltpu.make_async_remote_copy(
            src_ref=src,
            dst_ref=win[c].at[pl.ds(slot * block_rows + k * piece, piece)],
            send_sem=send_sem.at[flow, c, k],
            recv_sem=recv_sem.at[flow, c, k],
            device_id=device,
            device_id_type=MESH,
        )

    def own_piece(c, k):
        return feats.at[pl.ds(k * piece, piece), :, pl.ds(c * LANES, LANES)]

    def to_next(c, k):
        return remote(0, c, k, own_piece(c, k), 0, (me + 2, rep_next))

    def to_prev(c, k):
        return remote(1, c, k, own_piece(c, k), 4, (me - 2, rep_prev))

    def to_mate(c, k):
        return remote(2, c, k, own_piece(c, k), 1 + 2 * core, (mate, rep))

    def relay(c, k):
        start = (4 - 4 * core) * block_rows + k * piece
        return remote(3, c, k, win[c].at[pl.ds(start, piece)], 3 - 2 * core, (mate, rep))

    def arrived(flow, c, k):
        remote(flow, c, k, own_piece(c, k), 0, (mate, rep)).wait_recv()

    def part_copy(c, i):
        return pltpu.make_async_remote_copy(
            src_ref=partial_out.at[c, i],
            dst_ref=partial_in.at[c, i],
            send_sem=part_send.at[c, i],
            recv_sem=part_recv.at[c, i],
            device_id=(me, other),
            device_id_type=MESH,
        )

    degree_copy = pltpu.make_async_remote_copy(
        src_ref=degree_out,
        dst_ref=degree_in,
        send_sem=degree_sems.at[0],
        recv_sem=degree_sems.at[1],
        device_id=(me, other),
        device_id_type=MESH,
    )

    for c in range(chunks):
        own_copy(c).start()
    for b in range(block_rows):
        tile_copy(b).start()

    barrier = pltpu.get_barrier_semaphore()
    pl.semaphore_signal(barrier, inc=1, device_id=(mate, rep), device_id_type=MESH)
    pl.semaphore_signal(barrier, inc=1, device_id=(me, other), device_id_type=MESH)

    @pl.when(has_next)
    def _():
        pl.semaphore_signal(barrier, inc=1, device_id=(me + 2, rep_next), device_id_type=MESH)

    @pl.when(has_prev)
    def _():
        pl.semaphore_signal(barrier, inc=1, device_id=(me - 2, rep_prev), device_id_type=MESH)

    pl.semaphore_wait(barrier, 2 + has_next.astype(jnp.int32) + has_prev.astype(jnp.int32))

    for c in range(chunks):
        for k in range(PIECES):

            @pl.when(has_next)
            def _():
                to_next(c, k).start()

            @pl.when(has_prev)
            def _():
                to_prev(c, k).start()

            to_mate(c, k).start()

    lane = lax.broadcasted_iota(jnp.int32, (edge, LANES), 1)
    first_slot = rep * slots
    for c in range(chunks):
        win[c][zero_block] = jnp.zeros((edge, LANES), win[c].dtype)

    def within(s, used):
        return jnp.minimum(jnp.maximum(used - s, 0), 1)

    def degree_of(b, i, held):
        tile_copy(b).wait()
        used = live[0, b] - first_slot
        total = jnp.zeros((edge, edge), jnp.float32)
        for s in range(slots):
            total += tiles[b, s].astype(jnp.float32) * within(s, used).astype(jnp.float32)
        return jnp.where(lane == i, jnp.sum(total, axis=1, keepdims=True), held)

    no_degrees = jnp.zeros((edge, LANES), jnp.float32)
    degree_out[...] = lax.fori_loop(
        0, half, lambda i, held: degree_of(other * half + i, i, held), no_degrees
    )
    own_degrees = lax.fori_loop(
        0, half, lambda i, held: degree_of(rep * half + i, i, held), no_degrees
    )
    degree_copy.start()
    for c in range(chunks):
        own_copy(c).wait()

    @pl.loop(0, half)
    def _(i):
        block = REACH * block_rows + rep * half + i
        own = jnp.concatenate([win[c][block] for c in range(chunks)], axis=1)
        base[i] = jnp.dot(own, w_self[...], preferred_element_type=jnp.float32) + bias[...]

    degree_copy.wait()
    inverses = 1.0 / jnp.maximum(own_degrees + degree_in[...], 1.0)

    @pl.loop(0, half)
    def _(i):
        one = jnp.sum(jnp.where(lane == i, inverses, 0.0), axis=1, keepdims=True)
        inverse[i] = jnp.broadcast_to(one, (edge, LANES))

    def aggregate(c, b):
        used = live[0, b] - first_slot
        total = jnp.zeros((edge, LANES), jnp.float32)
        shift = (me - REACH) * block_rows

        def source(s):
            return win[c][zero_block + within(s, used) * (columns[b, s] - shift - zero_block)]

        for s in range(0, slots, 2):
            left = jnp.concatenate([tiles[b, s], tiles[b, s + 1]], axis=1)
            right = jnp.concatenate([source(s), source(s + 1)], axis=0)
            total += jnp.dot(left, right, preferred_element_type=jnp.float32)
        return total

    def finish(c, i):
        part_copy(c, i).wait_recv()
        total = own_totals[c, i] + partial_in[c, i].astype(jnp.float32)
        mean = (total * inverse[i]).astype(jnp.bfloat16)
        return base[i] + jnp.dot(
            mean, w_neigh[pl.ds(c * LANES, LANES), :], preferred_element_type=jnp.float32
        )

    for c in range(chunks):

        @pl.when(relay_out)
        def _():
            for k in range(PIECES):
                arrived(1 - core, c, k)
                relay(c, k).start()

        @pl.when(relay_in)
        def _():
            for k in range(PIECES):
                arrived(core, c, k)
                arrived(3, c, k)

        for k in range(PIECES):
            arrived(2, c, k)

        @pl.loop(0, half)
        def _(i):
            partial_out[c, i] = aggregate(c, other * half + i).astype(jnp.bfloat16)

            @pl.when(i > 0)
            def _():
                part_copy(c, i - 1).start()

        @pl.loop(0, half)
        def _(i):
            own_totals[c, i] = aggregate(c, rep * half + i)

            @pl.when(i == 0)
            def _():
                part_copy(c, half - 1).start()

        @pl.loop(0, half)
        def _(i):
            if c < chunks - 1:
                base[i] = finish(c, i)
            else:
                rows = pl.ds(pl.multiple_of(i * edge, edge), edge)
                out[rows, :] = jnp.maximum(finish(c, i), 0.0).astype(out.dtype)

    for c in range(chunks):
        for k in range(PIECES):

            @pl.when(has_next)
            def _():
                to_next(c, k).wait_send()

            @pl.when(has_prev)
            def _():
                to_prev(c, k).wait_send()

            to_mate(c, k).wait_send()

            @pl.when(relay_out)
            def _():
                relay(c, k).wait_send()

        @pl.loop(0, half)
        def _(i):
            part_copy(c, i).wait_send()


def local(row_total, features, adjacency, columns, live, w_self, w_neigh, bias):
    block_rows, slots, edge, _ = adjacency.shape
    node_rows, width = features.shape
    chunks, half = width // LANES, block_rows // 2
    dma = pltpu.SemaphoreType.DMA
    hbm = pl.BlockSpec(memory_space=pl.ANY)
    vmem = pl.BlockSpec(memory_space=pltpu.VMEM)
    smem = pl.BlockSpec(memory_space=pltpu.SMEM)
    window = pltpu.VMEM(((2 * REACH + 1) * block_rows + 1, edge, LANES), jnp.bfloat16)
    return pl.pallas_call(
        functools.partial(kernel, row_total),
        out_shape=jax.ShapeDtypeStruct((node_rows // 2, width), jnp.bfloat16),
        in_specs=[hbm, hbm, smem, smem, vmem, vmem, vmem],
        out_specs=vmem,
        scratch_shapes=[
            window,
            window,
            pltpu.VMEM(adjacency.shape, jnp.bfloat16),
            pltpu.VMEM((chunks, half, edge, LANES), jnp.bfloat16),
            pltpu.VMEM((chunks, half, edge, LANES), jnp.bfloat16),
            pltpu.VMEM((chunks, half, edge, LANES), jnp.float32),
            pltpu.VMEM((half, edge, width), jnp.float32),
            pltpu.VMEM((half, edge, LANES), jnp.float32),
            pltpu.VMEM((edge, LANES), jnp.float32),
            pltpu.VMEM((edge, LANES), jnp.float32),
            dma((block_rows,)),
            dma((chunks,)),
            dma((4, chunks, PIECES)),
            dma((4, chunks, PIECES)),
            dma((chunks, half)),
            dma((chunks, half)),
            dma((2,)),
        ],
        compiler_params=pltpu.CompilerParams(
            collective_id=0, has_side_effects=True, vmem_limit_bytes=60 << 20
        ),
    )(
        features.reshape(block_rows, edge, width), adjacency, columns, live.reshape(1, block_rows),
        w_self, w_neigh, bias.reshape(1, width),
    )


def solution(mesh):
    placed = (P("row", None), P("row", "rep", None, None), P("row", "rep"), P("row"), P(), P(), P())
    return jax.shard_map(
        functools.partial(local, mesh.shape["row"]),
        mesh=mesh, in_specs=placed, out_specs=P(("row", "rep"), None), check_vma=False,
    )
```

```python
import functools

import jax
import jax.numpy as jnp
from jax import lax
from jax.experimental import pallas as pl
from jax.experimental.pallas import tpu as pltpu
from jax.sharding import PartitionSpec as P

REACH = 2
LANES = 128
SHARED = (5, 3)
REST = ((3, 3), (5, 3, 2))
MESH = pl.DeviceIdType.MESH


def kernel(
    row_total, feats, adjacency, columns, live, w_self, w_neigh, bias, out,
    win_low, win_high, tiles, partial_out, partial_in, own_totals, base, inverse, degree_out, degree_in,
    tile_sem, own_sem, send_sem, recv_sem, part_send, part_recv, degree_sems,
):
    block_rows, slots, edge, _ = tiles.shape
    width = feats.shape[2]
    chunks = width // LANES
    half = block_rows // 2
    zero_block = (2 * REACH + 1) * block_rows
    win = (win_low, win_high)

    me = lax.axis_index("row")
    rep = lax.axis_index("rep")
    core = lax.rem(me, 2)
    mate = me + 1 - 2 * core
    other = 1 - rep
    has_next = me + 2 < row_total
    has_prev = me >= 2
    chip = me // 2
    middle = row_total // 4
    rep_next = jnp.where(chip == middle - 1, other, rep)
    rep_prev = jnp.where(chip == middle, other, rep)
    relay_out = jnp.where(core == 0, me + 2 < row_total, me >= 2)
    relay_in = jnp.where(core == 0, me >= 2, me + 2 < row_total)

    def tile_copy(b):
        return pltpu.make_async_copy(adjacency.at[b], tiles.at[b], tile_sem.at[b])

    def own_copy(c):
        return pltpu.make_async_copy(
            feats.at[:, :, pl.ds(c * LANES, LANES)],
            win[c].at[pl.ds(REACH * block_rows, block_rows)],
            own_sem.at[c],
        )

    def span(c, j, side):
        shared, rest = SHARED[c], REST[c]
        if j == 0:
            return (1 - side) * shared, shared
        if j <= len(rest):
            return 2 * shared + sum(rest[: j - 1]), rest[j - 1]
        return side * shared, shared

    def remote(flow, c, j, src, slot, start, size, device):
        return pltpu.make_async_remote_copy(
            src_ref=src,
            dst_ref=win[c].at[pl.ds(slot * block_rows + start, size)],
            send_sem=send_sem.at[flow, c, j],
            recv_sem=recv_sem.at[flow, c, j],
            device_id=device,
            device_id_type=MESH,
        )

    def own_piece(c, start, size):
        return feats.at[pl.ds(start, size), :, pl.ds(c * LANES, LANES)]

    def held(c, slot, start, size):
        return win[c].at[pl.ds(slot * block_rows + start, size)]

    def to_next(c, j):
        start, size = span(c, j, rep_next)
        return remote(0, c, j, own_piece(c, start, size), 0, start, size, (me + 2, rep_next))

    def to_prev(c, j):
        start, size = span(c, j, rep_prev)
        return remote(1, c, j, own_piece(c, start, size), 4, start, size, (me - 2, rep_prev))

    def to_mate(c):
        whole = own_piece(c, 0, block_rows)
        return remote(2, c, 0, whole, 1 + 2 * core, 0, block_rows, (mate, rep))

    def across(flow, c):
        start, size = span(c, 0, rep)
        j, slot = len(REST[c]) + 1, 4 * flow
        return remote(flow, c, j, held(c, slot, start, size), slot, start, size, (me, other))

    def relay(c, j):
        start, size = span(c, j, rep)
        src = held(c, 4 - 4 * core, start, size)
        return remote(3, c, j, src, 3 - 2 * core, start, size, (mate, rep))

    def arrived(flow, c, j):
        start, size = span(c, j, rep)
        remote(flow, c, j, held(c, 0, start, size), 0, start, size, (mate, rep)).wait_recv()

    def forward(c):
        @pl.when(relay_out)
        def _():
            arrived(1 - core, c, 0)
            across(1 - core, c).start()
            relay(c, 0).start()

        @pl.when(relay_in)
        def _():
            arrived(core, c, 0)
            across(core, c).start()

    def complete(c):
        last = len(REST[c])
        order = [*range(1, last), last + 1, last]

        @pl.when(relay_out)
        def _():
            for j in order:
                arrived(1 - core, c, j)
                relay(c, j).start()

        @pl.when(relay_in)
        def _():
            for j in order:
                arrived(core, c, j)
            for j in [0, *order]:
                arrived(3, c, j)

        to_mate(c).wait_recv()

    def part_copy(c, i):
        return pltpu.make_async_remote_copy(
            src_ref=partial_out.at[c, i],
            dst_ref=partial_in.at[c, i],
            send_sem=part_send.at[c, i],
            recv_sem=part_recv.at[c, i],
            device_id=(me, other),
            device_id_type=MESH,
        )

    degree_copy = pltpu.make_async_remote_copy(
        src_ref=degree_out,
        dst_ref=degree_in,
        send_sem=degree_sems.at[0],
        recv_sem=degree_sems.at[1],
        device_id=(me, other),
        device_id_type=MESH,
    )

    barrier = pltpu.get_barrier_semaphore()
    pl.semaphore_signal(barrier, inc=1, device_id=(mate, rep), device_id_type=MESH)
    pl.semaphore_signal(barrier, inc=1, device_id=(me, other), device_id_type=MESH)

    @pl.when(has_next)
    def _():
        pl.semaphore_signal(barrier, inc=1, device_id=(me + 2, rep_next), device_id_type=MESH)

    @pl.when(has_prev)
    def _():
        pl.semaphore_signal(barrier, inc=1, device_id=(me - 2, rep_prev), device_id_type=MESH)

    for c in range(chunks):
        own_copy(c).start()
    for b in range(block_rows):
        tile_copy(b).start()

    pl.semaphore_wait(barrier, 2 + has_next.astype(jnp.int32) + has_prev.astype(jnp.int32))

    for c in range(chunks):
        for j in range(len(REST[c]) + 1):

            @pl.when(has_next)
            def _():
                to_next(c, j).start()

            @pl.when(has_prev)
            def _():
                to_prev(c, j).start()

        to_mate(c).start()

    lane = lax.broadcasted_iota(jnp.int32, (edge, LANES), 1)
    first_slot = rep * slots
    for c in range(chunks):
        win[c][zero_block] = jnp.zeros((edge, LANES), win[c].dtype)

    def within(s, used):
        return jnp.minimum(jnp.maximum(used - s, 0), 1)

    def degree_of(b, i, found):
        tile_copy(b).wait()
        used = live[0, b] - first_slot
        total = jnp.zeros((edge, edge), jnp.float32)
        for s in range(slots):
            total += tiles[b, s].astype(jnp.float32) * within(s, used).astype(jnp.float32)
        return jnp.where(lane == i, jnp.sum(total, axis=1, keepdims=True), found)

    no_degrees = jnp.zeros((edge, LANES), jnp.float32)
    def packed(row):
        return jnp.transpose(row)[:half, :]

    degree_out[...] = packed(
        lax.fori_loop(0, half, lambda i, d: degree_of(other * half + i, i, d), no_degrees)
    )
    forward(0)
    own_degrees = lax.fori_loop(
        0, half, lambda i, d: degree_of(rep * half + i, i, d), no_degrees
    )
    degree_copy.start()
    for c in range(chunks):
        own_copy(c).wait()

    @pl.loop(0, half)
    def _(i):
        block = REACH * block_rows + rep * half + i
        own = jnp.concatenate([win[c][block] for c in range(chunks)], axis=1)
        base[i] = jnp.dot(own, w_self[...], preferred_element_type=jnp.float32) + bias[...]

    def aggregate(c, b):
        used = live[0, b] - first_slot
        total = jnp.zeros((edge, LANES), jnp.float32)
        shift = (me - REACH) * block_rows

        def source(s):
            return win[c][zero_block + within(s, used) * (columns[b, s] - shift - zero_block)]

        for s in range(0, slots, 2):
            left = jnp.concatenate([tiles[b, s], tiles[b, s + 1]], axis=1)
            right = jnp.concatenate([source(s), source(s + 1)], axis=0)
            total += jnp.dot(left, right, preferred_element_type=jnp.float32)
        return total

    def finish(c, i):
        part_copy(c, i).wait_recv()
        total = own_totals[c, i] + partial_in[c, i].astype(jnp.float32)
        mean = (total * inverse[i]).astype(jnp.bfloat16)
        return base[i] + jnp.dot(
            mean, w_neigh[pl.ds(c * LANES, LANES), :], preferred_element_type=jnp.float32
        )

    def send_partials(c):
        @pl.loop(0, half)
        def _(i):
            partial_out[c, i] = aggregate(c, other * half + i).astype(jnp.bfloat16)

            @pl.when(i > 0)
            def _():
                part_copy(c, i - 1).start()

    def keep_own(c):
        part_copy(c, half - 1).start()

        @pl.loop(0, half)
        def _(i):
            own_totals[c, i] = aggregate(c, rep * half + i)

    complete(0)
    send_partials(0)
    forward(1)
    keep_own(0)

    degree_copy.wait()
    others = jnp.concatenate(
        [degree_in[...], jnp.zeros((edge - half, LANES), jnp.float32)], axis=0
    )
    inverses = 1.0 / jnp.maximum(own_degrees + jnp.transpose(others), 1.0)

    @pl.loop(0, half)
    def _(i):
        one = jnp.sum(jnp.where(lane == i, inverses, 0.0), axis=1, keepdims=True)
        inverse[i] = jnp.broadcast_to(one, (edge, LANES))

    complete(1)
    send_partials(1)
    keep_own(1)

    @pl.loop(0, half)
    def _(i):
        base[i] = finish(0, i)

    @pl.loop(0, half)
    def _(i):
        rows = pl.ds(pl.multiple_of(i * edge, edge), edge)
        out[rows, :] = jnp.maximum(finish(1, i), 0.0).astype(out.dtype)

    for c in range(chunks):
        for j in range(len(REST[c]) + 1):

            @pl.when(has_next)
            def _():
                to_next(c, j).wait_send()

            @pl.when(has_prev)
            def _():
                to_prev(c, j).wait_send()

        to_mate(c).wait_send()

        @pl.when(has_prev)
        def _():
            across(0, c).wait_send()

        @pl.when(has_next)
        def _():
            across(1, c).wait_send()

        @pl.when(relay_out)
        def _():
            for j in range(len(REST[c]) + 2):
                relay(c, j).wait_send()

        @pl.loop(0, half)
        def _(i):
            part_copy(c, i).wait_send()


def local(row_total, features, adjacency, columns, live, w_self, w_neigh, bias):
    block_rows, slots, edge, _ = adjacency.shape
    node_rows, width = features.shape
    chunks, half = width // LANES, block_rows // 2
    pieces = 2 + max(len(rest) for rest in REST)
    dma = pltpu.SemaphoreType.DMA
    hbm = pl.BlockSpec(memory_space=pl.ANY)
    vmem = pl.BlockSpec(memory_space=pltpu.VMEM)
    smem = pl.BlockSpec(memory_space=pltpu.SMEM)
    window = pltpu.VMEM(((2 * REACH + 1) * block_rows + 1, edge, LANES), jnp.bfloat16)
    return pl.pallas_call(
        functools.partial(kernel, row_total),
        out_shape=jax.ShapeDtypeStruct((node_rows // 2, width), jnp.bfloat16),
        in_specs=[hbm, hbm, smem, smem, vmem, vmem, vmem],
        out_specs=vmem,
        scratch_shapes=[
            window,
            window,
            pltpu.VMEM(adjacency.shape, jnp.bfloat16),
            pltpu.VMEM((chunks, half, edge, LANES), jnp.bfloat16),
            pltpu.VMEM((chunks, half, edge, LANES), jnp.bfloat16),
            pltpu.VMEM((chunks, half, edge, LANES), jnp.float32),
            pltpu.VMEM((half, edge, width), jnp.float32),
            pltpu.VMEM((half, edge, LANES), jnp.float32),
            pltpu.VMEM((half, LANES), jnp.float32),
            pltpu.VMEM((half, LANES), jnp.float32),
            dma((block_rows,)),
            dma((chunks,)),
            dma((4, chunks, pieces)),
            dma((4, chunks, pieces)),
            dma((chunks, half)),
            dma((chunks, half)),
            dma((2,)),
        ],
        compiler_params=pltpu.CompilerParams(
            collective_id=0, has_side_effects=True, vmem_limit_bytes=60 << 20
        ),
    )(
        features.reshape(block_rows, edge, width), adjacency, columns, live.reshape(1, block_rows),
        w_self, w_neigh, bias.reshape(1, width),
    )


def solution(mesh):
    placed = (P("row", None), P("row", "rep", None, None), P("row", "rep"), P("row"), P(), P(), P())
    return jax.shard_map(
        functools.partial(local, mesh.shape["row"]),
        mesh=mesh, in_specs=placed, out_specs=P(("row", "rep"), None), check_vma=False,
    )
```

```python
import functools

import jax
import jax.numpy as jnp
from jax import lax
from jax.experimental import pallas as pl
from jax.experimental.pallas import tpu as pltpu
from jax.sharding import PartitionSpec as P

REACH = 2
LANES = 128
SHARED = ((2, 2), (2,))
REST = ((4, 3, 1), (4, 4, 3, 1))
MESH = pl.DeviceIdType.MESH


def kernel(
    row_total, feats, adjacency, columns, live, w_self, w_neigh, bias, out,
    win_low, win_high, tiles, partial_out, partial_in, own_totals, base, inverse, degree_out, degree_in,
    tile_sem, own_sem, send_sem, recv_sem, part_send, part_recv, degree_sems,
):
    block_rows, slots, edge, _ = tiles.shape
    width = feats.shape[2]
    chunks = width // LANES
    half = block_rows // 2
    zero_block = (2 * REACH + 1) * block_rows
    win = (win_low, win_high)

    me = lax.axis_index("row")
    rep = lax.axis_index("rep")
    core = lax.rem(me, 2)
    mate = me + 1 - 2 * core
    other = 1 - rep
    has_next = me + 2 < row_total
    has_prev = me >= 2
    chip = me // 2
    middle = row_total // 4
    rep_next = jnp.where(chip == middle - 1, other, rep)
    rep_prev = jnp.where(chip == middle, other, rep)
    relay_out = jnp.where(core == 0, me + 2 < row_total, me >= 2)
    relay_in = jnp.where(core == 0, me >= 2, me + 2 < row_total)

    def tile_copy(b):
        return pltpu.make_async_copy(adjacency.at[b], tiles.at[b], tile_sem.at[b])

    def own_copy(c):
        return pltpu.make_async_copy(
            feats.at[:, :, pl.ds(c * LANES, LANES)],
            win[c].at[pl.ds(REACH * block_rows, block_rows)],
            own_sem.at[c],
        )

    def span(c, j, side):
        shared, rest = SHARED[c], REST[c]
        count, total = len(shared), sum(shared)
        if j < count:
            return (1 - side) * total + sum(shared[:j]), shared[j]
        j -= count
        if j < len(rest):
            return 2 * total + sum(rest[:j]), rest[j]
        j -= len(rest)
        return side * total + sum(shared[:j]), shared[j]

    def remote(flow, c, j, src, slot, start, size, device):
        return pltpu.make_async_remote_copy(
            src_ref=src,
            dst_ref=win[c].at[pl.ds(slot * block_rows + start, size)],
            send_sem=send_sem.at[flow, c, j],
            recv_sem=recv_sem.at[flow, c, j],
            device_id=device,
            device_id_type=MESH,
        )

    def own_piece(c, start, size):
        return feats.at[pl.ds(start, size), :, pl.ds(c * LANES, LANES)]

    def held(c, slot, start, size):
        return win[c].at[pl.ds(slot * block_rows + start, size)]

    def to_next(c, j):
        start, size = span(c, j, rep_next)
        return remote(0, c, j, own_piece(c, start, size), 0, start, size, (me + 2, rep_next))

    def to_prev(c, j):
        start, size = span(c, j, rep_prev)
        return remote(1, c, j, own_piece(c, start, size), 4, start, size, (me - 2, rep_prev))

    def to_mate(c):
        whole = own_piece(c, 0, block_rows)
        return remote(2, c, 0, whole, 1 + 2 * core, 0, block_rows, (mate, rep))

    def across(flow, c, j):
        start, size = span(c, j, rep)
        slot = 4 * flow
        there = len(SHARED[c]) + len(REST[c]) + j
        return remote(flow, c, there, held(c, slot, start, size), slot, start, size, (me, other))

    def relay(c, j):
        start, size = span(c, j, rep)
        src = held(c, 4 - 4 * core, start, size)
        return remote(3, c, j, src, 3 - 2 * core, start, size, (mate, rep))

    def arrived(flow, c, j):
        start, size = span(c, j, rep)
        remote(flow, c, j, held(c, 0, start, size), 0, start, size, (mate, rep)).wait_recv()

    def direct(c):
        return range(len(SHARED[c]) + len(REST[c]))

    def forward(c):
        for j in range(len(SHARED[c])):

            @pl.when(relay_out)
            def _():
                arrived(1 - core, c, j)
                across(1 - core, c, j).start()
                relay(c, j).start()

            @pl.when(relay_in)
            def _():
                arrived(core, c, j)
                across(core, c, j).start()

    def pass_on(c, pieces):
        @pl.when(relay_out)
        def _():
            for j in pieces:
                arrived(1 - core, c, j)
                relay(c, j).start()

    def complete(c, passed):
        count, sent = len(SHARED[c]), len(direct(c))
        inbound = range(sent, sent + count)
        pass_on(c, [*range(count + passed, sent - 1), *inbound, sent - 1])

        @pl.when(relay_in)
        def _():
            for j in range(count, sent + count):
                arrived(core, c, j)
            for j in range(sent + count):
                arrived(3, c, j)

        to_mate(c).wait_recv()

    def part_copy(c, i):
        return pltpu.make_async_remote_copy(
            src_ref=partial_out.at[c, i],
            dst_ref=partial_in.at[c, i],
            send_sem=part_send.at[c, i],
            recv_sem=part_recv.at[c, i],
            device_id=(me, other),
            device_id_type=MESH,
        )

    degree_copy = pltpu.make_async_remote_copy(
        src_ref=degree_out,
        dst_ref=degree_in,
        send_sem=degree_sems.at[0],
        recv_sem=degree_sems.at[1],
        device_id=(me, other),
        device_id_type=MESH,
    )

    barrier = pltpu.get_barrier_semaphore()
    pl.semaphore_signal(barrier, inc=1, device_id=(mate, rep), device_id_type=MESH)
    pl.semaphore_signal(barrier, inc=1, device_id=(me, other), device_id_type=MESH)

    @pl.when(has_next)
    def _():
        pl.semaphore_signal(barrier, inc=1, device_id=(me + 2, rep_next), device_id_type=MESH)

    @pl.when(has_prev)
    def _():
        pl.semaphore_signal(barrier, inc=1, device_id=(me - 2, rep_prev), device_id_type=MESH)

    for c in range(chunks):
        own_copy(c).start()
    for b in range(block_rows):
        tile_copy(b).start()

    pl.semaphore_wait(barrier, 2 + has_next.astype(jnp.int32) + has_prev.astype(jnp.int32))

    for c in range(chunks):
        for j in direct(c):

            @pl.when(has_next)
            def _():
                to_next(c, j).start()

            @pl.when(has_prev)
            def _():
                to_prev(c, j).start()

        to_mate(c).start()

    lane = lax.broadcasted_iota(jnp.int32, (edge, LANES), 1)
    first_slot = rep * slots
    for c in range(chunks):
        win[c][zero_block] = jnp.zeros((edge, LANES), win[c].dtype)

    def within(s, used):
        return jnp.minimum(jnp.maximum(used - s, 0), 1)

    def degree_of(b, i, found):
        tile_copy(b).wait()
        used = live[0, b] - first_slot
        total = jnp.zeros((edge, edge), jnp.float32)
        for s in range(slots):
            total += tiles[b, s].astype(jnp.float32) * within(s, used).astype(jnp.float32)
        return jnp.where(lane == i, jnp.sum(total, axis=1, keepdims=True), found)

    no_degrees = jnp.zeros((edge, LANES), jnp.float32)
    def packed(row):
        return jnp.transpose(row)[:half, :]

    forward(0)
    degree_out[...] = packed(
        lax.fori_loop(0, half, lambda i, d: degree_of(other * half + i, i, d), no_degrees)
    )
    pass_on(0, [len(SHARED[0])])
    own_degrees = lax.fori_loop(
        0, half, lambda i, d: degree_of(rep * half + i, i, d), no_degrees
    )
    degree_copy.start()
    for c in range(chunks):
        own_copy(c).wait()

    @pl.loop(0, half)
    def _(i):
        block = REACH * block_rows + rep * half + i
        own = jnp.concatenate([win[c][block] for c in range(chunks)], axis=1)
        base[i] = jnp.dot(own, w_self[...], preferred_element_type=jnp.float32) + bias[...]

    def aggregate(c, b):
        used = live[0, b] - first_slot
        total = jnp.zeros((edge, LANES), jnp.float32)
        shift = (me - REACH) * block_rows

        def source(s):
            return win[c][zero_block + within(s, used) * (columns[b, s] - shift - zero_block)]

        for s in range(0, slots, 2):
            left = jnp.concatenate([tiles[b, s], tiles[b, s + 1]], axis=1)
            right = jnp.concatenate([source(s), source(s + 1)], axis=0)
            total += jnp.dot(left, right, preferred_element_type=jnp.float32)
        return total

    def finish(c, i):
        part_copy(c, i).wait_recv()
        total = own_totals[c, i] + partial_in[c, i].astype(jnp.float32)
        mean = (total * inverse[i]).astype(jnp.bfloat16)
        return base[i] + jnp.dot(
            mean, w_neigh[pl.ds(c * LANES, LANES), :], preferred_element_type=jnp.float32
        )

    def send_partials(c):
        @pl.loop(0, half)
        def _(i):
            partial_out[c, i] = aggregate(c, other * half + i).astype(jnp.bfloat16)

            @pl.when(i > 0)
            def _():
                part_copy(c, i - 1).start()

    def keep_own(c):
        part_copy(c, half - 1).start()

        @pl.loop(0, half)
        def _(i):
            own_totals[c, i] = aggregate(c, rep * half + i)

    complete(0, 1)
    forward(1)
    send_partials(0)
    keep_own(0)

    degree_copy.wait()
    others = jnp.concatenate(
        [degree_in[...], jnp.zeros((edge - half, LANES), jnp.float32)], axis=0
    )
    inverses = 1.0 / jnp.maximum(own_degrees + jnp.transpose(others), 1.0)

    @pl.loop(0, half)
    def _(i):
        one = jnp.sum(jnp.where(lane == i, inverses, 0.0), axis=1, keepdims=True)
        inverse[i] = jnp.broadcast_to(one, (edge, LANES))

    complete(1, 0)
    send_partials(1)
    keep_own(1)

    @pl.loop(0, half)
    def _(i):
        base[i] = finish(0, i)

    @pl.loop(0, half)
    def _(i):
        rows = pl.ds(pl.multiple_of(i * edge, edge), edge)
        out[rows, :] = jnp.maximum(finish(1, i), 0.0).astype(out.dtype)

    for c in range(chunks):
        for j in direct(c):

            @pl.when(has_next)
            def _():
                to_next(c, j).wait_send()

            @pl.when(has_prev)
            def _():
                to_prev(c, j).wait_send()

        to_mate(c).wait_send()

        @pl.when(has_prev)
        def _():
            for j in range(len(SHARED[c])):
                across(0, c, j).wait_send()

        @pl.when(has_next)
        def _():
            for j in range(len(SHARED[c])):
                across(1, c, j).wait_send()

        @pl.when(relay_out)
        def _():
            for j in range(len(SHARED[c]) + len(direct(c))):
                relay(c, j).wait_send()

        @pl.loop(0, half)
        def _(i):
            part_copy(c, i).wait_send()


def local(row_total, features, adjacency, columns, live, w_self, w_neigh, bias):
    block_rows, slots, edge, _ = adjacency.shape
    node_rows, width = features.shape
    chunks, half = width // LANES, block_rows // 2
    pieces = max(2 * len(a) + len(b) for a, b in zip(SHARED, REST))
    dma = pltpu.SemaphoreType.DMA
    hbm = pl.BlockSpec(memory_space=pl.ANY)
    vmem = pl.BlockSpec(memory_space=pltpu.VMEM)
    smem = pl.BlockSpec(memory_space=pltpu.SMEM)
    window = pltpu.VMEM(((2 * REACH + 1) * block_rows + 1, edge, LANES), jnp.bfloat16)
    return pl.pallas_call(
        functools.partial(kernel, row_total),
        out_shape=jax.ShapeDtypeStruct((node_rows // 2, width), jnp.bfloat16),
        in_specs=[hbm, hbm, smem, smem, vmem, vmem, vmem],
        out_specs=vmem,
        scratch_shapes=[
            window,
            window,
            pltpu.VMEM(adjacency.shape, jnp.bfloat16),
            pltpu.VMEM((chunks, half, edge, LANES), jnp.bfloat16),
            pltpu.VMEM((chunks, half, edge, LANES), jnp.bfloat16),
            pltpu.VMEM((chunks, half, edge, LANES), jnp.float32),
            pltpu.VMEM((half, edge, width), jnp.float32),
            pltpu.VMEM((half, edge, LANES), jnp.float32),
            pltpu.VMEM((half, LANES), jnp.float32),
            pltpu.VMEM((half, LANES), jnp.float32),
            dma((block_rows,)),
            dma((chunks,)),
            dma((4, chunks, pieces)),
            dma((4, chunks, pieces)),
            dma((chunks, half)),
            dma((chunks, half)),
            dma((2,)),
        ],
        compiler_params=pltpu.CompilerParams(
            collective_id=0, has_side_effects=True, vmem_limit_bytes=60 << 20
        ),
    )(
        features.reshape(block_rows, edge, width), adjacency, columns, live.reshape(1, block_rows),
        w_self, w_neigh, bias.reshape(1, width),
    )


def solution(mesh):
    placed = (P("row", None), P("row", "rep", None, None), P("row", "rep"), P("row"), P(), P(), P())
    return jax.shard_map(
        functools.partial(local, mesh.shape["row"]),
        mesh=mesh, in_specs=placed, out_specs=P(("row", "rep"), None), check_vma=False,
    )
```

```python
import functools

import jax
import jax.numpy as jnp
from jax import lax
from jax.experimental import pallas as pl
from jax.experimental.pallas import tpu as pltpu
from jax.sharding import PartitionSpec as P

REACH = 2
LANES = 128
SHARED = ((2, 2), (2,))
REST = ((4, 3, 1), (4, 4, 3, 1))
MESH = pl.DeviceIdType.MESH


def kernel(
    row_total, feats, adjacency, columns_hbm, live_hbm, w_self_hbm, w_neigh_hbm, bias_hbm, out_hbm,
    win_low, win_high, tiles, partial_out, partial_in, own_totals, base, inverse, degree_out, degree_in,
    tile_sem, own_sem, send_sem, recv_sem, part_send, part_recv, degree_sems,
    columns, live, w_self, w_neigh, bias, small_sem, out, out_sem,
):
    block_rows, slots, edge, _ = tiles.shape
    width = feats.shape[2]
    chunks = width // LANES
    half = block_rows // 2
    zero_block = (2 * REACH + 1) * block_rows
    win = (win_low, win_high)

    me = lax.axis_index("row")
    rep = lax.axis_index("rep")
    core = lax.rem(me, 2)
    mate = me + 1 - 2 * core
    other = 1 - rep
    has_next = me + 2 < row_total
    has_prev = me >= 2
    chip = me // 2
    middle = row_total // 4
    rep_next = jnp.where(chip == middle - 1, other, rep)
    rep_prev = jnp.where(chip == middle, other, rep)
    relay_out = jnp.where(core == 0, me + 2 < row_total, me >= 2)
    relay_in = jnp.where(core == 0, me >= 2, me + 2 < row_total)

    def tile_copy(b):
        return pltpu.make_async_copy(adjacency.at[b], tiles.at[b], tile_sem.at[b])

    def own_copy(c):
        return pltpu.make_async_copy(
            feats.at[:, :, pl.ds(c * LANES, LANES)],
            win[c].at[pl.ds(REACH * block_rows, block_rows)],
            own_sem.at[c],
        )

    def span(c, j, side):
        shared, rest = SHARED[c], REST[c]
        count, total = len(shared), sum(shared)
        if j < count:
            return (1 - side) * total + sum(shared[:j]), shared[j]
        j -= count
        if j < len(rest):
            return 2 * total + sum(rest[:j]), rest[j]
        j -= len(rest)
        return side * total + sum(shared[:j]), shared[j]

    def remote(flow, c, j, src, slot, start, size, device):
        return pltpu.make_async_remote_copy(
            src_ref=src,
            dst_ref=win[c].at[pl.ds(slot * block_rows + start, size)],
            send_sem=send_sem.at[flow, c, j],
            recv_sem=recv_sem.at[flow, c, j],
            device_id=device,
            device_id_type=MESH,
        )

    def own_piece(c, start, size):
        return feats.at[pl.ds(start, size), :, pl.ds(c * LANES, LANES)]

    def held(c, slot, start, size):
        return win[c].at[pl.ds(slot * block_rows + start, size)]

    def to_next(c, j):
        start, size = span(c, j, rep_next)
        return remote(0, c, j, own_piece(c, start, size), 0, start, size, (me + 2, rep_next))

    def to_prev(c, j):
        start, size = span(c, j, rep_prev)
        return remote(1, c, j, own_piece(c, start, size), 4, start, size, (me - 2, rep_prev))

    def to_mate(c):
        whole = own_piece(c, 0, block_rows)
        return remote(2, c, 0, whole, 1 + 2 * core, 0, block_rows, (mate, rep))

    def across(flow, c, j):
        start, size = span(c, j, rep)
        slot = 4 * flow
        there = len(SHARED[c]) + len(REST[c]) + j
        return remote(flow, c, there, held(c, slot, start, size), slot, start, size, (me, other))

    def relay(c, j):
        start, size = span(c, j, rep)
        src = held(c, 4 - 4 * core, start, size)
        return remote(3, c, j, src, 3 - 2 * core, start, size, (mate, rep))

    def arrived(flow, c, j):
        start, size = span(c, j, rep)
        remote(flow, c, j, held(c, 0, start, size), 0, start, size, (mate, rep)).wait_recv()

    def direct(c):
        return range(len(SHARED[c]) + len(REST[c]))

    def forward(c):
        for j in range(len(SHARED[c])):

            @pl.when(relay_out)
            def _():
                arrived(1 - core, c, j)
                across(1 - core, c, j).start()
                relay(c, j).start()

            @pl.when(relay_in)
            def _():
                arrived(core, c, j)
                across(core, c, j).start()

    def pass_on(c, pieces):
        @pl.when(relay_out)
        def _():
            for j in pieces:
                arrived(1 - core, c, j)
                relay(c, j).start()

    def complete(c, passed):
        count, sent = len(SHARED[c]), len(direct(c))
        inbound = range(sent, sent + count)
        pass_on(c, [*range(count + passed, sent - 1), *inbound, sent - 1])

        @pl.when(relay_in)
        def _():
            for j in range(count, sent + count):
                arrived(core, c, j)
            for j in range(sent + count):
                arrived(3, c, j)

        to_mate(c).wait_recv()

    def part_copy(c, i):
        return pltpu.make_async_remote_copy(
            src_ref=partial_out.at[c, i],
            dst_ref=partial_in.at[c, i],
            send_sem=part_send.at[c, i],
            recv_sem=part_recv.at[c, i],
            device_id=(me, other),
            device_id_type=MESH,
        )

    degree_copy = pltpu.make_async_remote_copy(
        src_ref=degree_out,
        dst_ref=degree_in,
        send_sem=degree_sems.at[0],
        recv_sem=degree_sems.at[1],
        device_id=(me, other),
        device_id_type=MESH,
    )

    small = [
        pltpu.make_async_copy(source, target, small_sem.at[n])
        for n, (source, target) in enumerate((
            (live_hbm, live), (columns_hbm, columns), (w_self_hbm, w_self), (w_neigh_hbm, w_neigh),
            (bias_hbm, bias),
        ))
    ]
    barrier = pltpu.get_barrier_semaphore()
    pl.semaphore_signal(barrier, inc=1, device_id=(mate, rep), device_id_type=MESH)
    pl.semaphore_signal(barrier, inc=1, device_id=(me, other), device_id_type=MESH)

    @pl.when(has_next)
    def _():
        pl.semaphore_signal(barrier, inc=1, device_id=(me + 2, rep_next), device_id_type=MESH)

    @pl.when(has_prev)
    def _():
        pl.semaphore_signal(barrier, inc=1, device_id=(me - 2, rep_prev), device_id_type=MESH)

    for c in range(chunks):
        own_copy(c).start()
    for copy in small:
        copy.start()
    for b in range(block_rows):
        tile_copy(b).start()

    pl.semaphore_wait(barrier, 2 + has_next.astype(jnp.int32) + has_prev.astype(jnp.int32))

    for c in range(chunks):
        for j in direct(c):

            @pl.when(has_next)
            def _():
                to_next(c, j).start()

            @pl.when(has_prev)
            def _():
                to_prev(c, j).start()

        to_mate(c).start()

    lane = lax.broadcasted_iota(jnp.int32, (edge, LANES), 1)
    first_slot = rep * slots
    for c in range(chunks):
        win[c][zero_block] = jnp.zeros((edge, LANES), win[c].dtype)

    def within(s, used):
        return jnp.minimum(jnp.maximum(used - s, 0), 1)

    def degree_of(b, i, found):
        tile_copy(b).wait()
        used = live[0, b] - first_slot
        total = jnp.zeros((edge, edge), jnp.float32)
        for s in range(slots):
            total += tiles[b, s].astype(jnp.float32) * within(s, used).astype(jnp.float32)
        return jnp.where(lane == i, jnp.sum(total, axis=1, keepdims=True), found)

    no_degrees = jnp.zeros((edge, LANES), jnp.float32)
    def packed(row):
        return jnp.transpose(row)[:half, :]

    forward(0)
    for copy in small:
        copy.wait()
    degree_out[...] = packed(
        lax.fori_loop(0, half, lambda i, d: degree_of(other * half + i, i, d), no_degrees)
    )
    pass_on(0, [len(SHARED[0])])
    own_degrees = lax.fori_loop(
        0, half, lambda i, d: degree_of(rep * half + i, i, d), no_degrees
    )
    degree_copy.start()
    for c in range(chunks):
        own_copy(c).wait()

    @pl.loop(0, half)
    def _(i):
        block = REACH * block_rows + rep * half + i
        own = jnp.concatenate([win[c][block] for c in range(chunks)], axis=1)
        base[i] = jnp.dot(own, w_self[...], preferred_element_type=jnp.float32) + bias[...]

    def aggregate(c, b):
        used = live[0, b] - first_slot
        total = jnp.zeros((edge, LANES), jnp.float32)
        shift = (me - REACH) * block_rows

        def source(s):
            return win[c][zero_block + within(s, used) * (columns[b, s] - shift - zero_block)]

        for s in range(0, slots, 2):
            left = jnp.concatenate([tiles[b, s], tiles[b, s + 1]], axis=1)
            right = jnp.concatenate([source(s), source(s + 1)], axis=0)
            total += jnp.dot(left, right, preferred_element_type=jnp.float32)
        return total

    def finish(c, i):
        part_copy(c, i).wait_recv()
        total = own_totals[c, i] + partial_in[c, i].astype(jnp.float32)
        mean = (total * inverse[i]).astype(jnp.bfloat16)
        return base[i] + jnp.dot(
            mean, w_neigh[pl.ds(c * LANES, LANES), :], preferred_element_type=jnp.float32
        )

    def send_partials(c):
        @pl.loop(0, half)
        def _(i):
            partial_out[c, i] = aggregate(c, other * half + i).astype(jnp.bfloat16)

            @pl.when(i > 0)
            def _():
                part_copy(c, i - 1).start()

    def keep_own(c):
        part_copy(c, half - 1).start()

        @pl.loop(0, half)
        def _(i):
            own_totals[c, i] = aggregate(c, rep * half + i)

    complete(0, 1)
    forward(1)
    send_partials(0)
    keep_own(0)

    degree_copy.wait()
    others = jnp.concatenate(
        [degree_in[...], jnp.zeros((edge - half, LANES), jnp.float32)], axis=0
    )
    inverses = 1.0 / jnp.maximum(own_degrees + jnp.transpose(others), 1.0)

    @pl.loop(0, half)
    def _(i):
        one = jnp.sum(jnp.where(lane == i, inverses, 0.0), axis=1, keepdims=True)
        inverse[i] = jnp.broadcast_to(one, (edge, LANES))

    complete(1, 0)
    send_partials(1)
    keep_own(1)

    @pl.loop(0, half)
    def _(i):
        base[i] = finish(0, i)

    def out_copy(i):
        rows = pl.ds(pl.multiple_of(i * edge, edge), edge)
        return pltpu.make_async_copy(out.at[rows], out_hbm.at[rows], out_sem.at[i])

    @pl.loop(0, half)
    def _(i):
        rows = pl.ds(pl.multiple_of(i * edge, edge), edge)
        out[rows, :] = jnp.maximum(finish(1, i), 0.0).astype(out.dtype)
        out_copy(i).start()

    for c in range(chunks):
        for j in direct(c):

            @pl.when(has_next)
            def _():
                to_next(c, j).wait_send()

            @pl.when(has_prev)
            def _():
                to_prev(c, j).wait_send()

        to_mate(c).wait_send()

        @pl.when(has_prev)
        def _():
            for j in range(len(SHARED[c])):
                across(0, c, j).wait_send()

        @pl.when(has_next)
        def _():
            for j in range(len(SHARED[c])):
                across(1, c, j).wait_send()

        @pl.when(relay_out)
        def _():
            for j in range(len(SHARED[c]) + len(direct(c))):
                relay(c, j).wait_send()

        @pl.loop(0, half)
        def _(i):
            part_copy(c, i).wait_send()

    @pl.loop(0, half)
    def _(i):
        out_copy(i).wait()


def local(row_total, features, adjacency, columns, live, w_self, w_neigh, bias):
    block_rows, slots, edge, _ = adjacency.shape
    node_rows, width = features.shape
    chunks, half = width // LANES, block_rows // 2
    pieces = max(2 * len(a) + len(b) for a, b in zip(SHARED, REST))
    dma = pltpu.SemaphoreType.DMA
    hbm = pl.BlockSpec(memory_space=pl.ANY)
    window = pltpu.VMEM(((2 * REACH + 1) * block_rows + 1, edge, LANES), jnp.bfloat16)
    return pl.pallas_call(
        functools.partial(kernel, row_total),
        out_shape=jax.ShapeDtypeStruct((node_rows // 2, width), jnp.bfloat16),
        in_specs=[hbm] * 7,
        out_specs=hbm,
        scratch_shapes=[
            window,
            window,
            pltpu.VMEM(adjacency.shape, jnp.bfloat16),
            pltpu.VMEM((chunks, half, edge, LANES), jnp.bfloat16),
            pltpu.VMEM((chunks, half, edge, LANES), jnp.bfloat16),
            pltpu.VMEM((chunks, half, edge, LANES), jnp.float32),
            pltpu.VMEM((half, edge, width), jnp.float32),
            pltpu.VMEM((half, edge, LANES), jnp.float32),
            pltpu.VMEM((half, LANES), jnp.float32),
            pltpu.VMEM((half, LANES), jnp.float32),
            dma((block_rows,)),
            dma((chunks,)),
            dma((4, chunks, pieces)),
            dma((4, chunks, pieces)),
            dma((chunks, half)),
            dma((chunks, half)),
            dma((2,)),
            pltpu.SMEM(columns.shape, jnp.int32),
            pltpu.SMEM((1, block_rows), jnp.int32),
            pltpu.VMEM(w_self.shape, w_self.dtype),
            pltpu.VMEM(w_neigh.shape, w_neigh.dtype),
            pltpu.VMEM((1, width), bias.dtype),
            dma((5,)),
            pltpu.VMEM((block_rows * edge // 2, width), jnp.bfloat16),
            dma((half,)),
        ],
        compiler_params=pltpu.CompilerParams(
            collective_id=0, has_side_effects=True, vmem_limit_bytes=60 << 20
        ),
    )(
        features.reshape(block_rows, edge, width), adjacency, columns, live.reshape(1, block_rows),
        w_self, w_neigh, bias.reshape(1, width),
    )


def solution(mesh):
    placed = (P("row", None), P("row", "rep", None, None), P("row", "rep"), P("row"), P(), P(), P())
    return jax.shard_map(
        functools.partial(local, mesh.shape["row"]),
        mesh=mesh, in_specs=placed, out_specs=P(("row", "rep"), None), check_vma=False,
    )
```

```python
import functools

import jax
import jax.numpy as jnp
from jax import lax
from jax.experimental import pallas as pl
from jax.experimental.pallas import tpu as pltpu
from jax.sharding import PartitionSpec as P

REACH = 2
LANES = 128
SHARED = ((2, 2), (2,))
REST = ((4, 3, 1), (4, 4, 3, 1))
MESH = pl.DeviceIdType.MESH


def kernel(
    row_total, feats, adjacency, columns_hbm, live_hbm, w_self_hbm, w_neigh_hbm, bias_hbm, out_hbm,
    win_low, win_high, tiles, partial_out, partial_in, own_totals, base, inverse, degree_out, degree_in,
    tile_sem, own_sem, send_sem, recv_sem, part_send, part_recv, degree_sems,
    columns, live, w_self, w_neigh, bias, small_sem, out, out_sem,
):
    block_rows, slots, edge, _ = tiles.shape
    width = feats.shape[2]
    chunks = width // LANES
    half = block_rows // 2
    zero_block = (2 * REACH + 1) * block_rows
    win = (win_low, win_high)

    me = lax.axis_index("row")
    rep = lax.axis_index("rep")
    core = lax.rem(me, 2)
    mate = me + 1 - 2 * core
    other = 1 - rep
    has_next = me + 2 < row_total
    has_prev = me >= 2
    chip = me // 2
    middle = row_total // 4
    rep_next = jnp.where(chip == middle - 1, other, rep)
    rep_prev = jnp.where(chip == middle, other, rep)
    relay_out = jnp.where(core == 0, me + 2 < row_total, me >= 2)
    relay_in = jnp.where(core == 0, me >= 2, me + 2 < row_total)

    def tile_copy(b):
        return pltpu.make_async_copy(adjacency.at[b], tiles.at[b], tile_sem.at[b])

    def own_copy(c):
        return pltpu.make_async_copy(
            feats.at[:, :, pl.ds(c * LANES, LANES)],
            win[c].at[pl.ds(REACH * block_rows, block_rows)],
            own_sem.at[c],
        )

    def span(c, j, side):
        shared, rest = SHARED[c], REST[c]
        count, total = len(shared), sum(shared)
        if j < count:
            return (1 - side) * total + sum(shared[:j]), shared[j]
        j -= count
        if j < len(rest):
            return 2 * total + sum(rest[:j]), rest[j]
        j -= len(rest)
        return side * total + sum(shared[:j]), shared[j]

    def remote(flow, c, j, src, slot, start, size, device):
        return pltpu.make_async_remote_copy(
            src_ref=src,
            dst_ref=win[c].at[pl.ds(slot * block_rows + start, size)],
            send_sem=send_sem.at[flow, c, j],
            recv_sem=recv_sem.at[flow, c, j],
            device_id=device,
            device_id_type=MESH,
        )

    def own_piece(c, start, size):
        return feats.at[pl.ds(start, size), :, pl.ds(c * LANES, LANES)]

    def held(c, slot, start, size):
        return win[c].at[pl.ds(slot * block_rows + start, size)]

    def to_next(c, j):
        start, size = span(c, j, rep_next)
        return remote(0, c, j, own_piece(c, start, size), 0, start, size, (me + 2, rep_next))

    def to_prev(c, j):
        start, size = span(c, j, rep_prev)
        return remote(1, c, j, own_piece(c, start, size), 4, start, size, (me - 2, rep_prev))

    def to_mate(c):
        whole = own_piece(c, 0, block_rows)
        return remote(2, c, 0, whole, 1 + 2 * core, 0, block_rows, (mate, rep))

    def across(flow, c, j):
        start, size = span(c, j, rep)
        slot = 4 * flow
        there = len(SHARED[c]) + len(REST[c]) + j
        return remote(flow, c, there, held(c, slot, start, size), slot, start, size, (me, other))

    def relay(c, j):
        start, size = span(c, j, rep)
        src = held(c, 4 - 4 * core, start, size)
        return remote(3, c, j, src, 3 - 2 * core, start, size, (mate, rep))

    def arrived(flow, c, j):
        start, size = span(c, j, rep)
        remote(flow, c, j, held(c, 0, start, size), 0, start, size, (mate, rep)).wait_recv()

    def direct(c):
        return range(len(SHARED[c]) + len(REST[c]))

    def forward(c):
        for j in range(len(SHARED[c])):

            @pl.when(relay_out)
            def _():
                arrived(1 - core, c, j)
                across(1 - core, c, j).start()
                relay(c, j).start()

            @pl.when(relay_in)
            def _():
                arrived(core, c, j)
                across(core, c, j).start()

    def pass_on(c, pieces):
        @pl.when(relay_out)
        def _():
            for j in pieces:
                arrived(1 - core, c, j)
                relay(c, j).start()

    def complete(c, passed):
        count, sent = len(SHARED[c]), len(direct(c))
        inbound = range(sent, sent + count)
        pass_on(c, [*range(count + passed, sent - 1), *inbound, sent - 1])

        @pl.when(relay_in)
        def _():
            for j in range(count, sent + count):
                arrived(core, c, j)
            for j in range(sent + count):
                arrived(3, c, j)

        to_mate(c).wait_recv()

    def part_copy(c, i):
        return pltpu.make_async_remote_copy(
            src_ref=partial_out.at[c, i],
            dst_ref=partial_in.at[c, i],
            send_sem=part_send.at[c, i],
            recv_sem=part_recv.at[c, i],
            device_id=(me, other),
            device_id_type=MESH,
        )

    degree_copy = pltpu.make_async_remote_copy(
        src_ref=degree_out,
        dst_ref=degree_in,
        send_sem=degree_sems.at[0],
        recv_sem=degree_sems.at[1],
        device_id=(me, other),
        device_id_type=MESH,
    )

    small = [
        pltpu.make_async_copy(source, target, small_sem.at[n])
        for n, (source, target) in enumerate((
            (live_hbm, live), (columns_hbm, columns), (w_self_hbm, w_self), (w_neigh_hbm, w_neigh),
            (bias_hbm, bias),
        ))
    ]
    barrier = pltpu.get_barrier_semaphore()

    @pl.when(has_next)
    def _():
        pl.semaphore_signal(barrier, inc=1, device_id=(me + 2, rep_next), device_id_type=MESH)

    @pl.when(has_prev)
    def _():
        pl.semaphore_signal(barrier, inc=1, device_id=(me - 2, rep_prev), device_id_type=MESH)

    pl.semaphore_signal(barrier, inc=1, device_id=(mate, rep), device_id_type=MESH)
    pl.semaphore_signal(barrier, inc=1, device_id=(me, other), device_id_type=MESH)

    pl.semaphore_wait(barrier, 2 + has_next.astype(jnp.int32) + has_prev.astype(jnp.int32))

    for c in range(chunks):
        for j in direct(c):

            @pl.when(has_next)
            def _():
                to_next(c, j).start()

            @pl.when(has_prev)
            def _():
                to_prev(c, j).start()

        to_mate(c).start()

    for c in range(chunks):
        own_copy(c).start()
    for copy in small:
        copy.start()
    for b in range(block_rows):
        tile_copy(b).start()

    lane = lax.broadcasted_iota(jnp.int32, (edge, LANES), 1)
    first_slot = rep * slots
    for c in range(chunks):
        win[c][zero_block] = jnp.zeros((edge, LANES), win[c].dtype)

    def within(s, used):
        return jnp.minimum(jnp.maximum(used - s, 0), 1)

    def degree_of(b, i, found):
        tile_copy(b).wait()
        used = live[0, b] - first_slot
        total = jnp.zeros((edge, edge), jnp.float32)
        for s in range(slots):
            total += tiles[b, s].astype(jnp.float32) * within(s, used).astype(jnp.float32)
        return jnp.where(lane == i, jnp.sum(total, axis=1, keepdims=True), found)

    no_degrees = jnp.zeros((edge, LANES), jnp.float32)
    def packed(row):
        return jnp.transpose(row)[:half, :]

    forward(0)
    for copy in small:
        copy.wait()
    degree_out[...] = packed(
        lax.fori_loop(0, half, lambda i, d: degree_of(other * half + i, i, d), no_degrees)
    )
    pass_on(0, [len(SHARED[0])])
    own_degrees = lax.fori_loop(
        0, half, lambda i, d: degree_of(rep * half + i, i, d), no_degrees
    )
    degree_copy.start()
    for c in range(chunks):
        own_copy(c).wait()

    @pl.loop(0, half)
    def _(i):
        block = REACH * block_rows + rep * half + i
        own = jnp.concatenate([win[c][block] for c in range(chunks)], axis=1)
        base[i] = jnp.dot(own, w_self[...], preferred_element_type=jnp.float32) + bias[...]

    def aggregate(c, b):
        used = live[0, b] - first_slot
        total = jnp.zeros((edge, LANES), jnp.float32)
        shift = (me - REACH) * block_rows

        def source(s):
            return win[c][zero_block + within(s, used) * (columns[b, s] - shift - zero_block)]

        for s in range(0, slots, 2):
            left = jnp.concatenate([tiles[b, s], tiles[b, s + 1]], axis=1)
            right = jnp.concatenate([source(s), source(s + 1)], axis=0)
            total += jnp.dot(left, right, preferred_element_type=jnp.float32)
        return total

    def finish(c, i):
        part_copy(c, i).wait_recv()
        total = own_totals[c, i] + partial_in[c, i].astype(jnp.float32)
        mean = (total * inverse[i]).astype(jnp.bfloat16)
        return base[i] + jnp.dot(
            mean, w_neigh[pl.ds(c * LANES, LANES), :], preferred_element_type=jnp.float32
        )

    def send_partials(c):
        @pl.loop(0, half)
        def _(i):
            partial_out[c, i] = aggregate(c, other * half + i).astype(jnp.bfloat16)

            @pl.when(i > 0)
            def _():
                part_copy(c, i - 1).start()

    def keep_own(c):
        part_copy(c, half - 1).start()

        @pl.loop(0, half)
        def _(i):
            own_totals[c, i] = aggregate(c, rep * half + i)

    complete(0, 1)
    forward(1)
    send_partials(0)
    keep_own(0)

    degree_copy.wait()
    others = jnp.concatenate(
        [degree_in[...], jnp.zeros((edge - half, LANES), jnp.float32)], axis=0
    )
    inverses = 1.0 / jnp.maximum(own_degrees + jnp.transpose(others), 1.0)

    @pl.loop(0, half)
    def _(i):
        one = jnp.sum(jnp.where(lane == i, inverses, 0.0), axis=1, keepdims=True)
        inverse[i] = jnp.broadcast_to(one, (edge, LANES))

    complete(1, 0)
    send_partials(1)
    keep_own(1)

    @pl.loop(0, half)
    def _(i):
        base[i] = finish(0, i)

    def out_copy(i):
        rows = pl.ds(pl.multiple_of(i * edge, edge), edge)
        return pltpu.make_async_copy(out.at[rows], out_hbm.at[rows], out_sem.at[i])

    @pl.loop(0, half)
    def _(i):
        rows = pl.ds(pl.multiple_of(i * edge, edge), edge)
        out[rows, :] = jnp.maximum(finish(1, i), 0.0).astype(out.dtype)
        out_copy(i).start()

    for c in range(chunks):
        for j in direct(c):

            @pl.when(has_next)
            def _():
                to_next(c, j).wait_send()

            @pl.when(has_prev)
            def _():
                to_prev(c, j).wait_send()

        to_mate(c).wait_send()

        @pl.when(has_prev)
        def _():
            for j in range(len(SHARED[c])):
                across(0, c, j).wait_send()

        @pl.when(has_next)
        def _():
            for j in range(len(SHARED[c])):
                across(1, c, j).wait_send()

        @pl.when(relay_out)
        def _():
            for j in range(len(SHARED[c]) + len(direct(c))):
                relay(c, j).wait_send()

        @pl.loop(0, half)
        def _(i):
            part_copy(c, i).wait_send()

    @pl.loop(0, half)
    def _(i):
        out_copy(i).wait()


def local(row_total, features, adjacency, columns, live, w_self, w_neigh, bias):
    block_rows, slots, edge, _ = adjacency.shape
    node_rows, width = features.shape
    chunks, half = width // LANES, block_rows // 2
    pieces = max(2 * len(a) + len(b) for a, b in zip(SHARED, REST))
    dma = pltpu.SemaphoreType.DMA
    hbm = pl.BlockSpec(memory_space=pl.ANY)
    window = pltpu.VMEM(((2 * REACH + 1) * block_rows + 1, edge, LANES), jnp.bfloat16)
    return pl.pallas_call(
        functools.partial(kernel, row_total),
        out_shape=jax.ShapeDtypeStruct((node_rows // 2, width), jnp.bfloat16),
        in_specs=[hbm] * 7,
        out_specs=hbm,
        scratch_shapes=[
            window,
            window,
            pltpu.VMEM(adjacency.shape, jnp.bfloat16),
            pltpu.VMEM((chunks, half, edge, LANES), jnp.bfloat16),
            pltpu.VMEM((chunks, half, edge, LANES), jnp.bfloat16),
            pltpu.VMEM((chunks, half, edge, LANES), jnp.float32),
            pltpu.VMEM((half, edge, width), jnp.float32),
            pltpu.VMEM((half, edge, LANES), jnp.float32),
            pltpu.VMEM((half, LANES), jnp.float32),
            pltpu.VMEM((half, LANES), jnp.float32),
            dma((block_rows,)),
            dma((chunks,)),
            dma((4, chunks, pieces)),
            dma((4, chunks, pieces)),
            dma((chunks, half)),
            dma((chunks, half)),
            dma((2,)),
            pltpu.SMEM(columns.shape, jnp.int32),
            pltpu.SMEM((1, block_rows), jnp.int32),
            pltpu.VMEM(w_self.shape, w_self.dtype),
            pltpu.VMEM(w_neigh.shape, w_neigh.dtype),
            pltpu.VMEM((1, width), bias.dtype),
            dma((5,)),
            pltpu.VMEM((block_rows * edge // 2, width), jnp.bfloat16),
            dma((half,)),
        ],
        compiler_params=pltpu.CompilerParams(
            collective_id=0, has_side_effects=True, vmem_limit_bytes=60 << 20
        ),
    )(
        features.reshape(block_rows, edge, width), adjacency, columns, live.reshape(1, block_rows),
        w_self, w_neigh, bias.reshape(1, width),
    )


def solution(mesh):
    placed = (P("row", None), P("row", "rep", None, None), P("row", "rep"), P("row"), P(), P(), P())
    return jax.shard_map(
        functools.partial(local, mesh.shape["row"]),
        mesh=mesh, in_specs=placed, out_specs=P(("row", "rep"), None), check_vma=False,
    )
```

```python
import functools

import jax
import jax.numpy as jnp
from jax import lax
from jax.experimental import pallas as pl
from jax.experimental.pallas import tpu as pltpu
from jax.sharding import PartitionSpec as P

REACH = 2
LANES = 128
SHARED = ((3,2),(2,))
REST = ((3,2,1),(7,4,1))
MESH = pl.DeviceIdType.MESH


def kernel(
    row_total, feats, adjacency, columns_hbm, live_hbm, w_self_hbm, w_neigh_hbm, bias_hbm, out_hbm,
    win_low, win_high, tiles, partial_out, partial_in, own_totals, base, inverse, degree_out, degree_in,
    tile_sem, own_sem, send_sem, recv_sem, part_send, part_recv, degree_sems,
    columns, live, w_self, w_neigh, bias, small_sem, out, out_sem,
):
    block_rows, slots, edge, _ = tiles.shape
    width = feats.shape[2]
    chunks = width // LANES
    half = block_rows // 2
    zero_block = (2 * REACH + 1) * block_rows
    win = (win_low, win_high)

    me = lax.axis_index("row")
    rep = lax.axis_index("rep")
    core = lax.rem(me, 2)
    mate = me + 1 - 2 * core
    other = 1 - rep
    has_next = me + 2 < row_total
    has_prev = me >= 2
    chip = me // 2
    middle = row_total // 4
    rep_next = jnp.where(chip == middle - 1, other, rep)
    rep_prev = jnp.where(chip == middle, other, rep)
    relay_out = jnp.where(core == 0, me + 2 < row_total, me >= 2)
    relay_in = jnp.where(core == 0, me >= 2, me + 2 < row_total)

    def tile_copy(b):
        return pltpu.make_async_copy(adjacency.at[b], tiles.at[b], tile_sem.at[b])

    def own_copy(c):
        return pltpu.make_async_copy(
            feats.at[:, :, pl.ds(c * LANES, LANES)],
            win[c].at[pl.ds(REACH * block_rows, block_rows)],
            own_sem.at[c],
        )

    def span(c, j, side):
        shared, rest = SHARED[c], REST[c]
        count, total = len(shared), sum(shared)
        if j < count:
            return (1 - side) * total + sum(shared[:j]), shared[j]
        j -= count
        if j < len(rest):
            return 2 * total + sum(rest[:j]), rest[j]
        j -= len(rest)
        return side * total + sum(shared[:j]), shared[j]

    def remote(flow, c, j, src, slot, start, size, device):
        return pltpu.make_async_remote_copy(
            src_ref=src,
            dst_ref=win[c].at[pl.ds(slot * block_rows + start, size)],
            send_sem=send_sem.at[flow, c, j],
            recv_sem=recv_sem.at[flow, c, j],
            device_id=device,
            device_id_type=MESH,
        )

    def own_piece(c, start, size):
        return feats.at[pl.ds(start, size), :, pl.ds(c * LANES, LANES)]

    def held(c, slot, start, size):
        return win[c].at[pl.ds(slot * block_rows + start, size)]

    def to_next(c, j):
        start, size = span(c, j, rep_next)
        return remote(0, c, j, own_piece(c, start, size), 0, start, size, (me + 2, rep_next))

    def to_prev(c, j):
        start, size = span(c, j, rep_prev)
        return remote(1, c, j, own_piece(c, start, size), 4, start, size, (me - 2, rep_prev))

    def to_mate(c):
        whole = own_piece(c, 0, block_rows)
        return remote(2, c, 0, whole, 1 + 2 * core, 0, block_rows, (mate, rep))

    def across(flow, c, j):
        start, size = span(c, j, rep)
        slot = 4 * flow
        there = len(SHARED[c]) + len(REST[c]) + j
        return remote(flow, c, there, held(c, slot, start, size), slot, start, size, (me, other))

    def relay(c, j):
        start, size = span(c, j, rep)
        src = held(c, 4 - 4 * core, start, size)
        return remote(3, c, j, src, 3 - 2 * core, start, size, (mate, rep))

    def arrived(flow, c, j):
        start, size = span(c, j, rep)
        remote(flow, c, j, held(c, 0, start, size), 0, start, size, (mate, rep)).wait_recv()

    def direct(c):
        return range(len(SHARED[c]) + len(REST[c]))

    def forward(c):
        for j in range(len(SHARED[c])):

            @pl.when(relay_out)
            def _():
                arrived(1 - core, c, j)
                across(1 - core, c, j).start()
                relay(c, j).start()

            @pl.when(relay_in)
            def _():
                arrived(core, c, j)
                across(core, c, j).start()

    def pass_on(c, pieces):
        @pl.when(relay_out)
        def _():
            for j in pieces:
                arrived(1 - core, c, j)
                relay(c, j).start()

    def complete(c, passed):
        count, sent = len(SHARED[c]), len(direct(c))
        inbound = range(sent, sent + count)
        pass_on(c, [*range(count + passed, sent - 1), *inbound, sent - 1])

        @pl.when(relay_in)
        def _():
            for j in range(count, sent + count):
                arrived(core, c, j)
            for j in range(sent + count):
                arrived(3, c, j)

        to_mate(c).wait_recv()

    def part_copy(c, i):
        return pltpu.make_async_remote_copy(
            src_ref=partial_out.at[c, i],
            dst_ref=partial_in.at[c, i],
            send_sem=part_send.at[c, i],
            recv_sem=part_recv.at[c, i],
            device_id=(me, other),
            device_id_type=MESH,
        )

    degree_copy = pltpu.make_async_remote_copy(
        src_ref=degree_out,
        dst_ref=degree_in,
        send_sem=degree_sems.at[0],
        recv_sem=degree_sems.at[1],
        device_id=(me, other),
        device_id_type=MESH,
    )

    small = [
        pltpu.make_async_copy(source, target, small_sem.at[n])
        for n, (source, target) in enumerate((
            (live_hbm, live), (columns_hbm, columns), (w_self_hbm, w_self), (w_neigh_hbm, w_neigh),
            (bias_hbm, bias),
        ))
    ]
    barrier = pltpu.get_barrier_semaphore()

    @pl.when(has_next)
    def _():
        pl.semaphore_signal(barrier, inc=1, device_id=(me + 2, rep_next), device_id_type=MESH)

    @pl.when(has_prev)
    def _():
        pl.semaphore_signal(barrier, inc=1, device_id=(me - 2, rep_prev), device_id_type=MESH)

    pl.semaphore_signal(barrier, inc=1, device_id=(mate, rep), device_id_type=MESH)
    pl.semaphore_signal(barrier, inc=1, device_id=(me, other), device_id_type=MESH)

    pl.semaphore_wait(barrier, 2 + has_next.astype(jnp.int32) + has_prev.astype(jnp.int32))

    for c in range(chunks):
        for j in direct(c):

            @pl.when(has_next)
            def _():
                to_next(c, j).start()

            @pl.when(has_prev)
            def _():
                to_prev(c, j).start()

        to_mate(c).start()

    for c in range(chunks):
        own_copy(c).start()
    for copy in small:
        copy.start()
    for b in range(block_rows):
        tile_copy(b).start()

    lane = lax.broadcasted_iota(jnp.int32, (edge, LANES), 1)
    first_slot = rep * slots
    for c in range(chunks):
        win[c][zero_block] = jnp.zeros((edge, LANES), win[c].dtype)

    def within(s, used):
        return jnp.minimum(jnp.maximum(used - s, 0), 1)

    def degree_of(b, i, found):
        tile_copy(b).wait()
        used = live[0, b] - first_slot
        total = jnp.zeros((edge, edge), jnp.float32)
        for s in range(slots):
            total += tiles[b, s].astype(jnp.float32) * within(s, used).astype(jnp.float32)
        return jnp.where(lane == i, jnp.sum(total, axis=1, keepdims=True), found)

    no_degrees = jnp.zeros((edge, LANES), jnp.float32)
    def packed(row):
        return jnp.transpose(row)[:half, :]

    forward(0)
    for copy in small:
        copy.wait()
    degree_out[...] = packed(
        lax.fori_loop(0, half, lambda i, d: degree_of(other * half + i, i, d), no_degrees)
    )
    pass_on(0, [len(SHARED[0])])
    own_degrees = lax.fori_loop(
        0, half, lambda i, d: degree_of(rep * half + i, i, d), no_degrees
    )
    degree_copy.start()
    for c in range(chunks):
        own_copy(c).wait()

    @pl.loop(0, half)
    def _(i):
        block = REACH * block_rows + rep * half + i
        own = jnp.concatenate([win[c][block] for c in range(chunks)], axis=1)
        base[i] = jnp.dot(own, w_self[...], preferred_element_type=jnp.float32) + bias[...]

    def aggregate(c, b):
        used = live[0, b] - first_slot
        total = jnp.zeros((edge, LANES), jnp.float32)
        shift = (me - REACH) * block_rows

        def source(s):
            return win[c][zero_block + within(s, used) * (columns[b, s] - shift - zero_block)]

        for s in range(0, slots, 2):
            left = jnp.concatenate([tiles[b, s], tiles[b, s + 1]], axis=1)
            right = jnp.concatenate([source(s), source(s + 1)], axis=0)
            total += jnp.dot(left, right, preferred_element_type=jnp.float32)
        return total

    def finish(c, i):
        part_copy(c, i).wait_recv()
        total = own_totals[c, i] + partial_in[c, i].astype(jnp.float32)
        mean = (total * inverse[i]).astype(jnp.bfloat16)
        return base[i] + jnp.dot(
            mean, w_neigh[pl.ds(c * LANES, LANES), :], preferred_element_type=jnp.float32
        )

    def send_partials(c):
        @pl.loop(0, half)
        def _(i):
            partial_out[c, i] = aggregate(c, other * half + i).astype(jnp.bfloat16)

            @pl.when(i > 0)
            def _():
                part_copy(c, i - 1).start()

    def keep_own(c):
        part_copy(c, half - 1).start()

        @pl.loop(0, half)
        def _(i):
            own_totals[c, i] = aggregate(c, rep * half + i)

    complete(0, 1)
    forward(1)
    send_partials(0)
    keep_own(0)

    degree_copy.wait()
    others = jnp.concatenate(
        [degree_in[...], jnp.zeros((edge - half, LANES), jnp.float32)], axis=0
    )
    inverses = 1.0 / jnp.maximum(own_degrees + jnp.transpose(others), 1.0)

    @pl.loop(0, half)
    def _(i):
        one = jnp.sum(jnp.where(lane == i, inverses, 0.0), axis=1, keepdims=True)
        inverse[i] = jnp.broadcast_to(one, (edge, LANES))

    complete(1, 0)
    send_partials(1)
    keep_own(1)

    @pl.loop(0, half)
    def _(i):
        base[i] = finish(0, i)

    def out_copy(i):
        rows = pl.ds(pl.multiple_of(i * edge, edge), edge)
        return pltpu.make_async_copy(out.at[rows], out_hbm.at[rows], out_sem.at[i])

    @pl.loop(0, half)
    def _(i):
        rows = pl.ds(pl.multiple_of(i * edge, edge), edge)
        out[rows, :] = jnp.maximum(finish(1, i), 0.0).astype(out.dtype)
        out_copy(i).start()

    for c in range(chunks):
        for j in direct(c):

            @pl.when(has_next)
            def _():
                to_next(c, j).wait_send()

            @pl.when(has_prev)
            def _():
                to_prev(c, j).wait_send()

        to_mate(c).wait_send()

        @pl.when(has_prev)
        def _():
            for j in range(len(SHARED[c])):
                across(0, c, j).wait_send()

        @pl.when(has_next)
        def _():
            for j in range(len(SHARED[c])):
                across(1, c, j).wait_send()

        @pl.when(relay_out)
        def _():
            for j in range(len(SHARED[c]) + len(direct(c))):
                relay(c, j).wait_send()

        @pl.loop(0, half)
        def _(i):
            part_copy(c, i).wait_send()

    @pl.loop(0, half)
    def _(i):
        out_copy(i).wait()


def local(row_total, features, adjacency, columns, live, w_self, w_neigh, bias):
    block_rows, slots, edge, _ = adjacency.shape
    node_rows, width = features.shape
    chunks, half = width // LANES, block_rows // 2
    pieces = max(2 * len(a) + len(b) for a, b in zip(SHARED, REST))
    dma = pltpu.SemaphoreType.DMA
    hbm = pl.BlockSpec(memory_space=pl.ANY)
    window = pltpu.VMEM(((2 * REACH + 1) * block_rows + 1, edge, LANES), jnp.bfloat16)
    return pl.pallas_call(
        functools.partial(kernel, row_total),
        out_shape=jax.ShapeDtypeStruct((node_rows // 2, width), jnp.bfloat16),
        in_specs=[hbm] * 7,
        out_specs=hbm,
        scratch_shapes=[
            window,
            window,
            pltpu.VMEM(adjacency.shape, jnp.bfloat16),
            pltpu.VMEM((chunks, half, edge, LANES), jnp.bfloat16),
            pltpu.VMEM((chunks, half, edge, LANES), jnp.bfloat16),
            pltpu.VMEM((chunks, half, edge, LANES), jnp.float32),
            pltpu.VMEM((half, edge, width), jnp.float32),
            pltpu.VMEM((half, edge, LANES), jnp.float32),
            pltpu.VMEM((half, LANES), jnp.float32),
            pltpu.VMEM((half, LANES), jnp.float32),
            dma((block_rows,)),
            dma((chunks,)),
            dma((4, chunks, pieces)),
            dma((4, chunks, pieces)),
            dma((chunks, half)),
            dma((chunks, half)),
            dma((2,)),
            pltpu.SMEM(columns.shape, jnp.int32),
            pltpu.SMEM((1, block_rows), jnp.int32),
            pltpu.VMEM(w_self.shape, w_self.dtype),
            pltpu.VMEM(w_neigh.shape, w_neigh.dtype),
            pltpu.VMEM((1, width), bias.dtype),
            dma((5,)),
            pltpu.VMEM((block_rows * edge // 2, width), jnp.bfloat16),
            dma((half,)),
        ],
        compiler_params=pltpu.CompilerParams(
            collective_id=0, has_side_effects=True, vmem_limit_bytes=60 << 20
        ),
    )(
        features.reshape(block_rows, edge, width), adjacency, columns, live.reshape(1, block_rows),
        w_self, w_neigh, bias.reshape(1, width),
    )


def solution(mesh):
    placed = (P("row", None), P("row", "rep", None, None), P("row", "rep"), P("row"), P(), P(), P())
    return jax.shard_map(
        functools.partial(local, mesh.shape["row"]),
        mesh=mesh, in_specs=placed, out_specs=P(("row", "rep"), None), check_vma=False,
    )
```
